32 devices in a mesh: curve: 32 (over z, y, x, core).
Axes of the slice: x: 2, y: 2, z: 4, core: 2. Of those that a mesh axis runs over, the one named last changes fastest.
Arguments:
- nodal_state: float32 [5, 64, 16384], P(None, None, 'curve'), may hold values from -9 to 9, as said below
- inverse_jacobian: float32 [16384], P('curve'), may hold values from 1 to 4
- speeds: float32 [3, 5], replicated, may hold values from -1.5 to 1.5
- refine_flags: int32 [16384], P('curve'), may hold values from 0 to 1, as said below
- send_index: int32 [12288], P('curve'), may hold values from 0 to 3071, as said below
- face_source: int32 [6, 16384], P(None, 'curve'), may hold values from 0 to 3455, as said below
Outputs:
- refined_state: float32 [5, 64, 30720], P(None, None, 'curve')
- refined_jacobian: float32 [30720], P('curve')
The draws below stay inside these ranges and needn't reach their ends.
Inputs may be any that keep to these rules, and one draw needn't show every extreme that they name: `nodal_state`: each element's 64 node values are a level plus a linear part plus noise of an amplitude that varies from element to element. `refine_flags`: exactly 64 flags per device on average over all devices, at most 128 on one device, a number that is reached; the refined elements of a device go only to itself and its two curve neighbours, at most 224 to each neighbour, a number that is reached. `send_index`: per device, four blocks of 96 entries for destination offsets -2, -1, 1, 2 along the curve (cyclically): entries f * 512 + n of the traces that device reads, in increasing order, then zeros in unused slots; the blocks for offsets -1 and 1 are always full. `face_source`: face pairing is symmetric: across face 2 d of an element lies face 2 d + 1 of its neighbour; neighbours are on the same device or on one within two curve offsets.
All inputs are finite; a program needn't handle non-finite values.
Results may differ from the reference program's by a relative error of at most 0.0003.
Values sent between devices are 32-bit elements; how exact they have to be, the bound alone decides.
A program may use at most 64 MiB of HBM per device.

```python
import math
import jax
import jax.numpy as jnp
import numpy as np
from jax import lax

VARS = 5
E_DEV = 512
FLAG_DEV = 64
HALO_W = 16
HALO_SLOTS = 96
ELEMS = 16384
NEW_ELEMS = 30720
N_CURVE = 32


def random_orders(key, count_rows, length):
    return jax.vmap(lambda single: jax.random.permutation(single, length))(jax.random.split(key, count_rows)).astype(jnp.int32)


def band_offsets(key, length, band_width):
    far_counts = jax.random.randint(key, (2,), 1, band_width + 1).astype(jnp.int32)
    edge_one = far_counts[0]
    edge_two = edge_one + band_width
    edge_three = edge_two + band_width
    edge_four = edge_three + far_counts[1]
    ranks = jnp.arange(length, dtype=jnp.int32)
    return jnp.where(ranks < edge_one, -2, jnp.where(ranks < edge_two, -1, jnp.where(ranks < edge_three, 1, jnp.where(ranks < edge_four, 2, 0)))).astype(jnp.int32)


def offset_slot(offset):
    return jnp.where(offset < 0, offset + 2, offset + 1).astype(jnp.int32)


def forest_tables(key):
    devices = N_CURVE
    elements = E_DEV
    slot_count = HALO_SLOTS
    base_key = jax.random.fold_in(key, 11)
    device_ids = jnp.arange(devices, dtype=jnp.int32)[:, None]
    neighbours = []
    for direction in range(3):
        dir_key = jax.random.fold_in(base_key, direction)
        first_key, second_key, band_key = jax.random.split(dir_key, 3)
        first = random_orders(first_key, devices, elements)
        second = random_orders(second_key, devices, elements)
        first_inverse = jnp.argsort(first, axis=1).astype(jnp.int32)
        second_inverse = jnp.argsort(second, axis=1).astype(jnp.int32)
        bands = band_offsets(band_key, elements, HALO_W)
        ahead = bands[first]
        target = (device_ids + ahead) % devices
        forward = target * elements + second[target, first]
        behind = bands[second_inverse]
        anchor = (device_ids - behind) % devices
        backward = anchor * elements + first_inverse[anchor, second_inverse]
        neighbours.append(forward)
        neighbours.append(backward)
    near_ids = jnp.stack(neighbours).astype(jnp.int32)
    owner = near_ids // elements
    relative = (owner - device_ids[None] + 2) % devices - 2
    slot_of = jnp.where(relative == 0, 4, offset_slot(relative)).astype(jnp.int32)
    flat_slot = jnp.transpose(slot_of, (1, 0, 2)).reshape(devices, 6 * elements)
    flat_ids = jnp.arange(6 * elements, dtype=jnp.int32)[None, :]
    sort_keys = flat_slot * (6 * elements) + flat_ids
    ordering = jnp.argsort(sort_keys, axis=1).astype(jnp.int32)
    position = jnp.argsort(ordering, axis=1).astype(jnp.int32)
    starts = jnp.stack([jnp.sum(flat_slot < block, axis=1) for block in range(4)], axis=1).astype(jnp.int32)
    counts = jnp.stack([jnp.sum(flat_slot == block, axis=1) for block in range(4)], axis=1).astype(jnp.int32)
    lanes = jnp.arange(slot_count, dtype=jnp.int32)
    picks = jnp.minimum(starts[:, :, None] + lanes[None, None, :], 6 * elements - 1)
    sent = jnp.take_along_axis(ordering, picks.reshape(devices, 4 * slot_count), axis=1).reshape(devices, 4, slot_count)
    sent = jnp.where(lanes[None, None, :] < counts[:, :, None], sent, 0).astype(jnp.int32)
    faces = jnp.arange(6, dtype=jnp.int32)[:, None, None]
    partner = faces + 1 - 2 * (faces % 2)
    sender_flat = partner * elements + near_ids % elements
    rank_at = position[owner, sender_flat] - starts[owner, offset_slot(-relative)]
    ghost_index = 6 * elements + offset_slot(relative) * slot_count + rank_at
    source = jnp.where(relative == 0, sender_flat, ghost_index).astype(jnp.int32)
    return (sent.reshape(-1), source.reshape(6, devices * elements))


def draw_send_index(key, part):
    return forest_tables(key)[0]


def draw_face_source(key, part):
    return forest_tables(key)[1]


def draw_refine_flags(key, part):
    devices = N_CURVE
    elements = E_DEV
    half_flags = FLAG_DEV // 2
    drift_key, spot_key, order_key = jax.random.split(jax.random.fold_in(key, 5), 3)
    drift_by = jax.random.randint(drift_key, (devices,), -half_flags, half_flags + 1).astype(jnp.int32)
    spot_at = jax.random.randint(spot_key, (), 1, devices - 1).astype(jnp.int32)
    device_ids = jnp.arange(devices, dtype=jnp.int32)
    drift_by = jnp.where(device_ids == spot_at - 1, -half_flags, drift_by)
    drift_by = jnp.where(device_ids == spot_at, half_flags, drift_by)
    drift_by = jnp.where(device_ids == devices - 1, 0, drift_by).astype(jnp.int32)
    before = jnp.concatenate([jnp.zeros((1,), jnp.int32), drift_by[:-1]])
    counts = FLAG_DEV + drift_by - before
    orders = random_orders(order_key, devices, elements)
    return (orders < counts[:, None]).astype(jnp.int32).reshape(-1)


def draw_nodal_state(key, part):
    first_key, second_key, third_key, fourth_key = jax.random.split(jax.random.fold_in(key, 3), 4)
    element_total = ELEMS
    root = 1.0 / math.sqrt(5.0)
    points = jnp.array([-1.0, -root, root, 1.0], jnp.float32)
    node_ids = jnp.arange(64, dtype=jnp.int32)
    node_positions = jnp.stack([points[node_ids % 4], points[node_ids // 4 % 4], points[node_ids // 16]])
    level = 0.6 * jax.random.truncated_normal(first_key, -3.0, 3.0, (5, 1, element_total), jnp.float32)
    gradient_slopes = 0.4 * jax.random.truncated_normal(second_key, -3.0, 3.0, (5, 3, element_total), jnp.float32)
    incline_factor = jnp.einsum('whz,hq->wqz', gradient_slopes, node_positions)
    rough = jnp.exp(jax.random.uniform(third_key, (1, 1, element_total), jnp.float32, math.log(0.03), 0.0))
    noise = jax.random.truncated_normal(fourth_key, -3.0, 3.0, (5, 64, element_total), jnp.float32)
    return (level + incline_factor + rough * noise).astype(jnp.float32)


def level_of(rng, shape, cuts, smallest, top_value):
    def one(dim, parts):
        draws = jax.random.uniform(jax.random.fold_in(jax.random.fold_in(rng, 6), dim), (parts,), jnp.float32, smallest / len(cuts), top_value / len(cuts))
        return jnp.repeat(jnp.exp(draws), shape[dim] // parts).reshape((-1,) + (1,) * (len(shape) - dim - 1))

    level = one(*cuts[0])
    for cut in cuts[1:]:
        level = level * one(*cut)
    return level


def setup_inputs(seed: int = 0) -> dict:
    streams_of = jax.random.split(jax.random.key(seed), 7)
    return {
        "nodal_state": draw_nodal_state(jax.random.fold_in(streams_of[6], 71), 0),
        "inverse_jacobian": jnp.clip(jnp.exp(math.log(4.0) - 1.3862944 * jax.random.uniform(streams_of[1], (ELEMS,), jnp.float32) ** level_of(streams_of[1], (ELEMS,), ((0, 32),), -0.2, 0.2)), 1.0, 4.0),
        "speeds": jnp.clip(jax.random.uniform(streams_of[2], (3, VARS), jnp.float32, -1.5, 1.5), -1.5, 1.5),
        "refine_flags": draw_refine_flags(jax.random.fold_in(streams_of[6], 71), 0),
        "send_index": draw_send_index(jax.random.fold_in(streams_of[6], 71), 0),
        "face_source": draw_face_source(jax.random.fold_in(streams_of[6], 71), 0),
    }


time_step = 0.02

def lagrange_at(points, targets):
    values_at = np.ones((len(targets), 4))
    for basis_id in range(4):
        for partner in range(4):
            if partner != basis_id:
                values_at[:, basis_id] *= (targets - points[partner]) / (points[basis_id] - points[partner])
    return values_at

def modes_table(points):
    mono_to_legendre = np.array([[1.0, 0.0, 0.0, 0.0], [0.0, 1.0, 0.0, 0.0], [1.0 / 3.0, 0.0, 2.0 / 3.0, 0.0], [0.0, 0.6, 0.0, 0.4]])
    table = np.zeros((4, 4))
    for basis_id in range(4):
        coef = [1.0, 0.0, 0.0, 0.0]
        for partner in range(4):
            if partner != basis_id:
                denom = points[basis_id] - points[partner]
                fresh = [0.0, 0.0, 0.0, 0.0]
                for power in range(4):
                    lower = coef[power - 1] if power > 0 else 0.0
                    fresh[power] = (lower - points[partner] * coef[power]) / denom
                coef = fresh
        legendre = np.zeros(4)
        for power in range(4):
            legendre = legendre + coef[power] * mono_to_legendre[power]
        table[:, basis_id] = legendre
    return table

def node_constants():
    root = 1.0 / math.sqrt(5.0)
    points = np.array([-1.0, -root, root, 1.0])
    weights = np.array([1.0, 5.0, 5.0, 1.0]) / 6.0
    barycentric = np.ones(4)
    for node_row in range(4):
        for node_col in range(4):
            if node_row != node_col:
                barycentric[node_row] /= points[node_row] - points[node_col]
    deriv = np.zeros((4, 4))
    for node_row in range(4):
        for node_col in range(4):
            if node_row != node_col:
                deriv[node_row, node_col] = barycentric[node_col] / barycentric[node_row] / (points[node_row] - points[node_col])
        deriv[node_row, node_row] = -np.sum(deriv[node_row])
    to_modes = modes_table(points)
    sides = [lagrange_at(points, (points - 1.0) / 2.0), lagrange_at(points, (points + 1.0) / 2.0)]
    prolong = np.stack([np.kron(sides[child_id >> 2 & 1], np.kron(sides[child_id >> 1 & 1], sides[child_id & 1])) for child_id in range(8)])
    degrees = np.arange(4)
    levels = np.maximum(np.maximum(degrees[:, None, None], degrees[None, :, None]), degrees[None, None, :])
    top_mask = np.where(levels == 3, 1.0, 0.0)
    return (jnp.asarray(deriv, jnp.float32), jnp.asarray(weights, jnp.float32), jnp.asarray(to_modes, jnp.float32), jnp.asarray(prolong, jnp.float32), jnp.asarray(top_mask, jnp.float32))

def apply_along(matrix, values, node_axis):
    forms = {1: 'ak,vkjie->vajie', 2: 'aj,vkjie->vkaie', 3: 'ai,vkjie->vkjae'}
    return jnp.einsum(forms[node_axis], matrix, values, precision=lax.Precision.HIGHEST)

def face_flux(left_side, right_side, speed_dim):
    central = speed_dim * (left_side * left_side + left_side * right_side + right_side * right_side) / 6.0
    reach_by = jnp.abs(speed_dim) * jnp.maximum(jnp.abs(left_side), jnp.abs(right_side))
    return central - 0.5 * reach_by * (right_side - left_side)

def face_traces(shaped):
    element_count = shaped.shape[4]
    layers = []
    for dim_id in range(3):
        node_axis = 3 - dim_id
        for side_at in (0, 3):
            layers.append(lax.slice_in_dim(shaped, side_at, side_at + 1, axis=node_axis).reshape(5, 16, element_count))
    return jnp.stack(layers, axis=2)

def section_update(shaped, outside, speeds, inverse_jacobian):
    deriv, weights, to_modes, prolong, top_mask = node_constants()
    modal_coef = apply_along(to_modes, apply_along(to_modes, apply_along(to_modes, shaped[0:1], 1), 2), 3)[0]
    energy = modal_coef * modal_coef
    high_part = lax.optimization_barrier(jnp.sum(energy * top_mask[:, :, :, None], axis=(0, 1, 2)))
    all_part = lax.optimization_barrier(jnp.sum(energy, axis=(0, 1, 2)))
    top_ratio = high_part / (all_part + 1e-06)
    blend_weight = 0.5 * top_ratio / (top_ratio + 0.1)
    high_rate = jnp.zeros_like(shaped)
    lower_order_rate = jnp.zeros_like(shaped)
    for dim_id in range(3):
        node_axis = 3 - dim_id
        shape_w = [1, 1, 1, 1, 1]
        shape_w[node_axis] = 4
        node_weights = weights.reshape(shape_w)
        speed_dim = speeds[dim_id].reshape(5, 1, 1, 1, 1)
        volume = -(speed_dim / 3.0) * (shaped * apply_along(deriv, shaped, node_axis) + apply_along(deriv, shaped * shaped, node_axis))
        first_layer = lax.slice_in_dim(shaped, 0, 1, axis=node_axis)
        last_layer = lax.slice_in_dim(shaped, 3, 4, axis=node_axis)
        outer_left = outside[:, :, 2 * dim_id, :].reshape(first_layer.shape)
        outer_right = outside[:, :, 2 * dim_id + 1, :].reshape(first_layer.shape)
        flux_left = face_flux(outer_left, first_layer, speed_dim)
        flux_right = face_flux(last_layer, outer_right, speed_dim)
        middle = jnp.zeros_like(lax.slice_in_dim(shaped, 1, 3, axis=node_axis))
        surface_terms = jnp.concatenate([6.0 * (flux_left - 0.5 * speed_dim * first_layer * first_layer), middle, -6.0 * (flux_right - 0.5 * speed_dim * last_layer * last_layer)], axis=node_axis)
        inner_flux = face_flux(lax.slice_in_dim(shaped, 0, 3, axis=node_axis), lax.slice_in_dim(shaped, 1, 4, axis=node_axis), speed_dim)
        fluxes = jnp.concatenate([flux_left, inner_flux, flux_right], axis=node_axis)
        low_dim = -(lax.slice_in_dim(fluxes, 1, 5, axis=node_axis) - lax.slice_in_dim(fluxes, 0, 4, axis=node_axis)) / node_weights
        high_rate = high_rate + volume + surface_terms
        lower_order_rate = lower_order_rate + low_dim
    rate_all = inverse_jacobian * ((1.0 - blend_weight) * high_rate + blend_weight * lower_order_rate)
    return shaped + time_step * rate_all

def refine_block(updated, jacobian, flag_ids, flag_most):
    deriv, weights, to_modes, prolong, top_mask = node_constants()
    element_count = updated.shape[2]
    capacity = element_count + 7 * flag_most
    flag_ids = flag_ids.astype(jnp.int32)
    before = jnp.cumsum(flag_ids).astype(jnp.int32) - flag_ids
    element_ids = jnp.arange(element_count, dtype=jnp.int32)
    slot_ids = jnp.where(flag_ids == 1, before, flag_most).astype(jnp.int32)
    listing = jnp.zeros((flag_most,), jnp.int32).at[slot_ids].set(element_ids, mode='drop')
    chosen = jnp.take(updated, listing, axis=2)
    stacked = jnp.transpose(chosen, (1, 0, 2)).reshape(64, 5 * flag_most)
    children = jnp.dot(prolong.reshape(512, 64), stacked, precision=lax.Precision.HIGHEST, preferred_element_type=jnp.float32)
    children = jnp.transpose(children.reshape(8, 64, 5, flag_most), (2, 1, 0, 3)).reshape(5, 64, 8 * flag_most)
    placed = element_ids + 7 * before
    updated_refine_marks = jnp.zeros((capacity,), jnp.int32).at[placed].add(1)
    parent = jnp.clip(jnp.cumsum(updated_refine_marks).astype(jnp.int32) - 1, 0, element_count - 1)
    new_ids = jnp.arange(capacity, dtype=jnp.int32)
    child_id = new_ids - placed[parent]
    parent_flag = flag_ids[parent]
    new_total = (element_count + 7 * jnp.sum(flag_ids)).astype(jnp.int32)
    source = jnp.where(parent_flag == 1, element_count + child_id * flag_most + before[parent], parent)
    source = jnp.where(new_ids < new_total, source, 0).astype(jnp.int32)
    refined = jnp.take(jnp.concatenate([updated, children], axis=2), source, axis=2)
    new_jac = jacobian[parent] * jnp.where(parent_flag == 1, 2.0, 1.0).astype(jacobian.dtype)
    return (refined, new_jac, new_total)

def reference(nodal_state, inverse_jacobian, speeds, refine_flags, send_index, face_source):
    devices = N_CURVE
    elements = E_DEV
    slot_count = HALO_SLOTS
    element_total = devices * elements
    shaped = nodal_state.reshape(5, 4, 4, 4, element_total)
    traces = face_traces(shaped)
    trace_table = jnp.transpose(traces.reshape(5, 16, 6, devices, elements), (0, 1, 3, 2, 4)).reshape(5, 16, devices * 6 * elements)
    receiver = (jnp.arange(element_total, dtype=jnp.int32) // elements)[None, :]
    ghost_id = face_source - 6 * elements
    place_id = jnp.clip(ghost_id // slot_count, 0, 3)
    lane_id = jnp.clip(ghost_id - place_id * slot_count, 0, slot_count - 1)
    shifts = jnp.array([-2, -1, 1, 2], jnp.int32)
    sender = (receiver + shifts[place_id]) % devices
    blocks = send_index.reshape(devices, 4, slot_count)
    sent_flat = blocks[sender, 3 - place_id, lane_id]
    global_ids = jnp.where(face_source < 6 * elements, receiver * 6 * elements + face_source, sender * 6 * elements + sent_flat).astype(jnp.int32)
    outside = jnp.take(trace_table, global_ids.reshape(-1), axis=2).reshape(5, 16, 6, element_total)
    updated = section_update(shaped, outside, speeds, inverse_jacobian).reshape(5, 64, element_total)
    refined, new_jac, new_total = refine_block(updated, inverse_jacobian, refine_flags, FLAG_DEV * devices)
    return (refined[:, :, :NEW_ELEMS], new_jac[:NEW_ELEMS])
```

```python
import functools
import math

import jax
import jax.numpy as jnp
import numpy as np
from jax import lax
from jax.experimental import pallas as pl
from jax.experimental.pallas import tpu as pltpu
from jax.sharding import PartitionSpec as P

FLAG_MOST = 128
E_NEW = 960
EDGE = 256
SLOT = 128

time_step = 0.02
F32 = jnp.float32
BF16 = jnp.bfloat16
MESH = pl.DeviceIdType.MESH


def lagrange_at(points, targets):
    values_at = np.ones((len(targets), 4))
    for basis_id in range(4):
        for partner in range(4):
            if partner != basis_id:
                values_at[:, basis_id] *= (targets - points[partner]) / (
                    points[basis_id] - points[partner]
                )
    return values_at


def modes_table(points):
    mono_to_legendre = np.array(
        [
            [1.0, 0.0, 0.0, 0.0],
            [0.0, 1.0, 0.0, 0.0],
            [1.0 / 3.0, 0.0, 2.0 / 3.0, 0.0],
            [0.0, 0.6, 0.0, 0.4],
        ]
    )
    table = np.zeros((4, 4))
    for basis_id in range(4):
        coef = [1.0, 0.0, 0.0, 0.0]
        for partner in range(4):
            if partner != basis_id:
                denom = points[basis_id] - points[partner]
                fresh = [0.0, 0.0, 0.0, 0.0]
                for power in range(4):
                    lower = coef[power - 1] if power > 0 else 0.0
                    fresh[power] = (lower - points[partner] * coef[power]) / denom
                coef = fresh
        legendre = np.zeros(4)
        for power in range(4):
            legendre = legendre + coef[power] * mono_to_legendre[power]
        table[:, basis_id] = legendre
    return table


def halves_np(values):
    high = np.asarray(values, np.float32).astype(BF16)
    low = (np.asarray(values, np.float32) - high.astype(np.float32)).astype(BF16)
    return high, low


def wide_np(values):
    high, low = halves_np(values)
    return np.concatenate([high, low, high], axis=1)


def constants():
    root = 1.0 / math.sqrt(5.0)
    points = np.array([-1.0, -root, root, 1.0])
    barycentric = np.ones(4)
    for row in range(4):
        for col in range(4):
            if row != col:
                barycentric[row] /= points[row] - points[col]
    deriv = np.zeros((4, 4))
    for row in range(4):
        for col in range(4):
            if row != col:
                deriv[row, col] = (
                    barycentric[col] / barycentric[row] / (points[row] - points[col])
                )
        deriv[row, row] = -np.sum(deriv[row])
    eye = np.eye(4)
    along = [
        np.kron(eye, np.kron(eye, deriv)),
        np.kron(eye, np.kron(deriv, eye)),
        np.kron(deriv, np.kron(eye, eye)),
    ]
    nodes = np.arange(64)
    volume_u, volume_sq = [], []
    for d in range(3):
        place = nodes // 4**d % 4
        ends = np.diag(3.0 * (place == 3) - 3.0 * (place == 0))
        volume_u.append(-along[d] / 3.0)
        volume_sq.append(-along[d] / 3.0 + ends)
    to_modes = modes_table(points)
    modal = np.kron(to_modes, np.kron(to_modes, to_modes))
    sides = [lagrange_at(points, (points - 1.0) / 2.0), lagrange_at(points, (points + 1.0) / 2.0)]
    prolong = np.concatenate(
        [
            np.kron(sides[c >> 2 & 1], np.kron(sides[c >> 1 & 1], sides[c & 1]))
            for c in range(8)
        ]
    )
    pick = np.zeros((480, 320), np.float32)
    for f in range(6):
        face_nodes = nodes[nodes // 4 ** (f // 2) % 4 == (3 if f % 2 else 0)]
        for v in range(5):
            for at, node in enumerate(face_nodes):
                pick[f * 80 + v * 16 + at, v * 64 + node] = 1.0
    return (
        np.stack(volume_u).astype(np.float32),
        np.stack(volume_sq).astype(np.float32),
        wide_np(modal),
        wide_np(prolong),
        pick.astype(BF16),
        np.ascontiguousarray(pick.T).astype(BF16),
    )


def halves(values):
    high = values.astype(BF16)
    return high, (values - high.astype(F32)).astype(BF16)


def dot(left, right):
    return jnp.dot(left, right, preferred_element_type=F32)


def dot_t(left, right):
    return lax.dot_general(left, right, (((1,), (1,)), ((), ())), preferred_element_type=F32)


def ones_where(condition):
    return jnp.where(condition, 1.0, 0.0).astype(BF16)


def iota(shape, dim):
    return lax.broadcasted_iota(jnp.int32, shape, dim)


def face_flux(left, right, a, abs_a):
    central = (a / 6.0) * (left * (left + right) + right * right)
    return central - (0.5 * abs_a) * jnp.maximum(jnp.abs(left), jnp.abs(right)) * (right - left)


def tall(values):
    high, low = halves(values)
    return jnp.concatenate([high, high, low], axis=0)


def kernel(
    peers, slots,
    u_ref, jac_ref, speeds_ref, flags_ref, send_ref, source_ref,
    vol_u_ref, vol_sq_ref, modal_ref, prolong_ref, pick_ref, place_ref,
    out_ref, out_jac_ref,
    trace_ref, halo_out, halo_in, hot_ref, outside_ref, base_ref, table_ref, edge_out, edge_in,
    count_out, count_in,
    halo_send, halo_recv, edge_send, edge_recv, count_send, count_recv,
):
    count = u_ref.shape[1]
    me = lax.axis_index("curve")

    def peer(by):
        return lax.rem(me + by + peers, peers)

    barrier = pltpu.get_barrier_semaphore()

    def greet(by, carry):
        pl.semaphore_signal(barrier, inc=1, device_id=(peer(by),), device_id_type=MESH)
        return carry

    lax.fori_loop(1, peers, greet, 0)

    flag_rows = jnp.broadcast_to(flags_ref[...].astype(F32), (SLOT, count)).astype(BF16)
    row_id = iota((count, count), 0)
    col_id = iota((count, count), 1)
    before_col = dot_t(ones_where(col_id < row_id), flag_rows)
    upto_col = dot_t(ones_where(col_id <= row_id), flag_rows)
    before_row = dot(flag_rows, ones_where(row_id < col_id))
    flagged_col = (upto_col - before_col) > 0.5
    total_flags = upto_col[count - 1 : count, :]
    count_out[...] = count + 7.0 * total_flags

    u_high, u_low = halves(u_ref[...])
    pick = pick_ref[...]
    trace_ref[0] = dot(pick, u_high).astype(BF16)
    trace_ref[1] = dot(pick, u_low).astype(BF16)
    wanted = send_ref[...]
    entry = iota((count, SLOT), 0)
    for o in range(4):
        for f in range(6):
            hot_ref[f * count : (f + 1) * count, o * SLOT : (o + 1) * SLOT] = ones_where(
                entry + f * count == wanted[o : o + 1, :]
            )
    total = jnp.zeros((80, 4 * SLOT), F32)
    for f in range(6):
        hot = hot_ref[f * count : (f + 1) * count, :]
        total = total + dot(trace_ref[0, f * 80 : (f + 1) * 80, :], hot)
        total = total + dot(trace_ref[1, f * 80 : (f + 1) * 80, :], hot)
    for o in range(4):
        halo_out[o] = total[:, o * SLOT : (o + 1) * SLOT]

    pl.semaphore_wait(barrier, peers - 1)

    halo_copies = []
    for b, by in enumerate((-2, -1, 1, 2)):
        copy = pltpu.make_async_remote_copy(
            src_ref=halo_out.at[b],
            dst_ref=halo_in.at[3 - b],
            send_sem=halo_send.at[b],
            recv_sem=halo_recv.at[3 - b],
            device_id=(peer(by),),
            device_id_type=MESH,
        )
        copy.start()
        halo_copies.append(copy)

    def tell(by, carry):
        pltpu.make_async_remote_copy(
            src_ref=count_out,
            dst_ref=count_in.at[me],
            send_sem=count_send,
            recv_sem=count_recv,
            device_id=(peer(by),),
            device_id_type=MESH,
        ).start()
        return carry

    lax.fori_loop(1, peers, tell, 0)

    jac = jac_ref[...]
    modal = dot(modal_ref[...], tall(u_ref[0:64, :]))
    energy = modal * modal
    node = iota((64, count), 0)
    at_end = [((node >> (2 * d)) & 3) for d in range(3)]
    top = (at_end[0] == 3) | (at_end[1] == 3) | (at_end[2] == 3)
    high_part = jnp.sum(jnp.where(top, energy, 0.0), axis=0, keepdims=True)
    all_part = jnp.sum(energy, axis=0, keepdims=True)
    ratio = high_part / (all_part + 1e-06)
    blend = 0.5 * ratio / (ratio + 0.1)
    scale = time_step * jac
    for v in range(5):
        u = u_ref[v * 64 : (v + 1) * 64, :]
        w_u = jnp.zeros((64, 64), F32)
        w_sq = jnp.zeros((64, 64), F32)
        low = jnp.zeros((64, count), F32)
        for d in range(3):
            a = speeds_ref[d, v]
            w_u = w_u + a * vol_u_ref[d]
            w_sq = w_sq + a * vol_sq_ref[d]
            step = 4**d
            flux = face_flux(u, pltpu.roll(u, 64 - step, 0), a, jnp.abs(a))
            flux = jnp.where(at_end[d] < 3, flux, 0.0)
            inv_w = jnp.where((at_end[d] == 0) | (at_end[d] == 3), 6.0, 1.2)
            low = low + inv_w * (pltpu.roll(flux, step, 0) - flux)

        def wide(w):
            high, small = halves(w)
            return jnp.concatenate([high, small, high], axis=1)

        high = u * dot(wide(w_u), tall(u)) + dot(wide(w_sq), tall(u * u))
        base_ref[v * 64 : (v + 1) * 64, :] = u + scale * (high + blend * (low - high))

    entry = iota((count, count), 0)
    for f in range(6):
        partner = f + 1 - 2 * (f % 2)
        hot = ones_where(entry + partner * count == source_ref[f : f + 1, :])
        outside_ref[f * 80 : (f + 1) * 80, :] = dot(
            trace_ref[0, partner * 80 : (partner + 1) * 80, :], hot
        ) + dot(trace_ref[1, partner * 80 : (partner + 1) * 80, :], hot)

    placed_col = iota((count, SLOT), 0).astype(F32) + 7.0 * before_col
    nowhere = -1.0e6
    single_at = jnp.where(flagged_col, nowhere, placed_col)
    chosen = ones_where(flagged_col & (before_col == iota((count, SLOT), 1).astype(F32)))
    flag_row_f = flag_rows.astype(F32)
    chosen_t = ones_where(
        (flag_row_f > 0.5) & (before_row == iota((FLAG_MOST, count), 0).astype(F32))
    )
    coarse = jnp.floor(placed_col * 0.0625)
    fine = placed_col - 16.0 * coarse
    family_at = 16.0 * dot(chosen_t, coarse.astype(BF16)) + dot(chosen_t, fine.astype(BF16))
    family_at = jnp.where(
        iota((FLAG_MOST, SLOT), 0).astype(F32) < total_flags, family_at, nowhere
    )

    for copy in halo_copies:
        copy.wait()
    ghosts = [halves(halo_in[b]) for b in range(4)]
    ghost_high = jnp.concatenate([g[0] for g in ghosts], axis=1)
    ghost_low = jnp.concatenate([g[1] for g in ghosts], axis=1)
    at = iota((4 * SLOT, count), 0)
    ghost_id = jnp.where(
        at % SLOT < slots, 6 * count + (at // SLOT) * slots + at % SLOT, -1
    )
    for f in range(6):
        d = f // 2
        hot = ones_where(ghost_id == source_ref[f : f + 1, :])
        outer = (
            outside_ref[f * 80 : (f + 1) * 80, :] + dot(ghost_high, hot) + dot(ghost_low, hot)
        )
        inner = trace_ref[0, f * 80 : (f + 1) * 80, :].astype(F32) + trace_ref[
            1, f * 80 : (f + 1) * 80, :
        ].astype(F32)
        for v in range(5):
            a = speeds_ref[d, v]
            left, right = outer[v * 16 : (v + 1) * 16, :], inner[v * 16 : (v + 1) * 16, :]
            if f % 2:
                left, right = right, left
            flux = face_flux(left, right, a, jnp.abs(a))
            sign = -6.0 if f % 2 else 6.0
            outside_ref[f * 80 + v * 16 : f * 80 + (v + 1) * 16, :] = (sign * scale) * flux
    change_high, change_low = halves(outside_ref[...])
    place = place_ref[...]
    updated = base_ref[...] + dot(place, change_high) + dot(place, change_low)

    extra = jnp.where(iota((16, count), 0) == 0, jnp.broadcast_to(jac, (16, count)), 0.0)
    up_high, up_low = halves(updated)
    ex_high, ex_low = halves(extra)
    table_ref[0:320, 0:count] = up_high
    table_ref[320:336, 0:count] = ex_high
    table_ref[336:656, 0:count] = up_low
    table_ref[656:672, 0:count] = ex_low
    parents = dot(table_ref[0:336, 0:count], chosen) + dot(table_ref[336:672, 0:count], chosen)
    stacked = jnp.concatenate([parents[v * 64 : (v + 1) * 64, :] for v in range(5)], axis=1)
    children = dot(prolong_ref[...], tall(stacked))
    child_high, child_low = halves(children)
    jac_high, jac_low = halves(2.0 * parents[320:336, :])
    for c in range(8):
        lanes = pl.ds(count + c * FLAG_MOST, FLAG_MOST)
        for v in range(5):
            block = (slice(c * 64, (c + 1) * 64), slice(v * FLAG_MOST, (v + 1) * FLAG_MOST))
            table_ref[v * 64 : (v + 1) * 64, lanes] = child_high[block]
            table_ref[336 + v * 64 : 336 + (v + 1) * 64, lanes] = child_low[block]
        table_ref[320:336, lanes] = jac_high
        table_ref[656:672, lanes] = jac_low

    whole = pltpu.make_async_remote_copy(
        src_ref=count_in.at[pl.ds(0, peers - 1)],
        dst_ref=count_in.at[pl.ds(0, peers - 1)],
        send_sem=count_send,
        recv_sem=count_recv,
        device_id=(peer(1),),
        device_id_type=MESH,
    )
    whole.wait()
    counts = count_in[...].reshape(peers, SLOT)
    start = jnp.sum(jnp.where(iota((peers, SLOT), 0) < me, counts, 0.0), axis=0, keepdims=True)
    first = (me * E_NEW).astype(F32) - start

    def gathered(places, width):
        rows = jnp.broadcast_to(places, (count, width))
        own = jnp.concatenate([single_at] * (width // SLOT), axis=1)
        family = jnp.concatenate([family_at] * (width // SLOT), axis=1)
        hot_ref[0:count, 0:width] = ones_where(rows == own)
        for c in range(8):
            begin = count + c * FLAG_MOST
            hot_ref[begin : begin + FLAG_MOST, 0:width] = ones_where(
                rows[0:FLAG_MOST, :] == family + float(c)
            )
        hot = hot_ref[0 : count + 8 * FLAG_MOST, 0:width]
        return dot(table_ref[0:336, :], hot) + dot(table_ref[336:672, :], hot)

    tail = E_NEW // EDGE * EDGE
    rest = E_NEW - tail
    lane = iota((1, EDGE), 1)
    offset = jnp.concatenate([first] * (EDGE // SLOT), axis=1)
    edge_copies = []
    for side, by in enumerate((1, -1)):
        if side == 0:
            there = lane + E_NEW
        else:
            there = jnp.where(lane < rest, tail + lane, tail - EDGE + lane) - E_NEW
        edge_out[side] = gathered(offset + there.astype(F32), EDGE)[0:328, :]
        copy = pltpu.make_async_remote_copy(
            src_ref=edge_out.at[side],
            dst_ref=edge_in.at[side],
            send_sem=edge_send.at[side],
            recv_sem=edge_recv.at[side],
            device_id=(peer(by),),
            device_id_type=MESH,
        )
        copy.start()
        edge_copies.append(copy)
    for begin in range(0, E_NEW, EDGE):
        width = min(EDGE, E_NEW - begin)
        values = gathered(offset + (lane + begin).astype(F32), EDGE)
        out_ref[:, begin : begin + width] = values[0:320, 0:width]
        out_jac_ref[:, begin : begin + width] = values[320:321, 0:width]
    for copy in edge_copies:
        copy.wait()
    out_ref[:, 0:EDGE] += edge_in[0, 0:320, :]
    out_jac_ref[:, 0:EDGE] += edge_in[0, 320:321, :]
    out_ref[:, tail:E_NEW] += edge_in[1, 0:320, 0:rest]
    out_jac_ref[:, tail:E_NEW] += edge_in[1, 320:321, 0:rest]
    begin = rest // SLOT * SLOT
    keep = iota((320, EDGE - begin), 1) + begin >= rest
    last = edge_in[1, :, begin:EDGE]
    lanes = slice(tail - EDGE + begin, tail)
    out_ref[:, lanes] += jnp.where(keep, last[0:320, :], 0.0)
    out_jac_ref[:, lanes] += jnp.where(keep[0:1, :], last[320:321, :], 0.0)


def solution(mesh):
    peers = mesh.shape["curve"]
    tables = constants()

    def shards(nodal_state, inverse_jacobian, speeds, refine_flags, send_index, face_source):
        count = nodal_state.shape[2]
        slots = send_index.shape[0] // 4
        wanted = jnp.pad(send_index.reshape(4, slots), ((0, 0), (0, SLOT - slots)))
        vmem = pl.BlockSpec(memory_space=pltpu.VMEM)
        smem = pl.BlockSpec(memory_space=pltpu.SMEM)
        hot_rows = max(6 * count, count + 8 * FLAG_MOST)
        refined, jac = pl.pallas_call(
            functools.partial(kernel, peers, slots),
            out_shape=(
                jax.ShapeDtypeStruct((320, E_NEW), F32),
                jax.ShapeDtypeStruct((1, E_NEW), F32),
            ),
            in_specs=[vmem, vmem, smem] + [vmem] * 9,
            out_specs=(vmem, vmem),
            scratch_shapes=[
                pltpu.VMEM((2, 480, count), BF16),
                pltpu.VMEM((4, 80, SLOT), F32),
                pltpu.VMEM((4, 80, SLOT), F32),
                pltpu.VMEM((hot_rows, 4 * SLOT), BF16),
                pltpu.VMEM((480, count), F32),
                pltpu.VMEM((320, count), F32),
                pltpu.VMEM((672, count + 8 * FLAG_MOST), BF16),
                pltpu.VMEM((2, 328, EDGE), F32),
                pltpu.VMEM((2, 328, EDGE), F32),
                pltpu.VMEM((1, SLOT), F32),
                pltpu.VMEM((peers, 1, SLOT), F32),
                pltpu.SemaphoreType.DMA((4,)),
                pltpu.SemaphoreType.DMA((4,)),
                pltpu.SemaphoreType.DMA((2,)),
                pltpu.SemaphoreType.DMA((2,)),
                pltpu.SemaphoreType.DMA,
                pltpu.SemaphoreType.DMA,
            ],
            compiler_params=pltpu.CompilerParams(
                collective_id=0, has_side_effects=True, vmem_limit_bytes=60 * 1024 * 1024
            ),
        )(
            nodal_state.reshape(320, count),
            inverse_jacobian.reshape(1, count),
            speeds,
            refine_flags.reshape(1, count),
            wanted,
            face_source,
            *[jnp.asarray(table) for table in tables],
        )
        return refined.reshape(5, 64, E_NEW), jac.reshape(E_NEW)

    return jax.shard_map(
        shards,
        mesh=mesh,
        in_specs=(
            P(None, None, "curve"),
            P("curve"),
            P(),
            P("curve"),
            P("curve"),
            P(None, "curve"),
        ),
        out_specs=(P(None, None, "curve"), P("curve")),
        check_vma=False,
    )
```
